256 devices in a mesh: space: 32 (over x, z_hi, core), member: 4 (over y), window: 2 (over z_lo).
Axes of the slice: x: 4, y: 4, z: 8 (z_hi: 4, z_lo: 2; z = z_hi * 2 + z_lo), core: 2. Of those that a mesh axis runs over, the one named last changes fastest.
Arguments:
- initial_replica_fields: float32 [2, 64, 512, 512], P('window', 'member', 'space'), may hold values from -6 to 6
- sensor_jitter: float32 [2, 2, 64, 512, 512], P('window', None, 'member', 'space'), may hold values from -6 to 6
- measurements: float32 [2, 2, 512, 512], P('window', None, 'space'), may hold values from -6 to 6
- measured_indicator: int32 [2, 2, 512, 512], P('window', None, 'space'), may hold values 0 or 1
- sensor_error_power: float32 [512, 512], P('space'), may hold values from 4096 to 40960
- adjacent_tiles: int32 [512, 4], P('space'), may hold values from 0 to 511, as said below
- coupling_operators: bfloat16 [4, 512, 512], replicated, may hold values from -0.125 to 0.125
- analysis_cotangent: float32 [2, 64, 512, 512], P('window', 'member', 'space'), may hold values from -6 to 6
Outputs:
- weight_grad: float32 [4, 512, 512], P(None, 'space')
- initial_grad: float32 [2, 64, 512, 512], P('window', 'member', 'space')
The draws below stay inside these ranges and needn't reach their ends.
Inputs may be any that keep to these rules, and one draw needn't show every extreme that they name: `adjacent_tiles`: neighbour k of block b is block (b + o) mod 512 with -2 <= o <= 2; slot 0 is b itself; distances -2 and 2 both occur.
All inputs are finite; a program needn't handle non-finite values. No bound on the sum of `measured_indicator` on one device may be relied on, other than what follows from the above.
Results may differ from the reference program's by a relative error of at most 0.0045.
Values may be sent and summed in bfloat16 or wider, within the bound.
No kernel may reach another device: no remote copies, remote signals or barrier semaphores. Data moves between devices by JAX's collectives and lax.ppermute only.
A program may use at most 128 MiB of HBM per device.

```python
import math
import jax
import jax.numpy as jnp
from jax import lax

BLOCK_CELLS = 512
NEIGHBOUR_SLOTS = 4
BLOCK_RADIUS = 2
CYCLES = 2
REPLICA_TALLY = 64
GRAPH_BLOCKS = 512
WIN = 2


def draw_adjacent_tiles(key, part):
    block_offsets = jax.random.randint(key, (GRAPH_BLOCKS, NEIGHBOUR_SLOTS), -BLOCK_RADIUS, BLOCK_RADIUS + 1, dtype=jnp.int32)
    block_offsets = block_offsets.at[:, 0].set(0)
    block_offsets = block_offsets.at[0, 1].set(-BLOCK_RADIUS)
    block_offsets = block_offsets.at[0, 2].set(BLOCK_RADIUS)
    block_offsets = block_offsets.at[0, 3].set(-1)
    blocks = jnp.arange(GRAPH_BLOCKS, dtype=jnp.int32)[:, None]
    return (blocks + block_offsets) % GRAPH_BLOCKS


def set_ends(values, key, low, high):
    longest = values.shape.index(max(values.shape))
    spots = []
    for shift in (0, 1):
        where = [jax.random.randint(jax.random.fold_in(key, axis), (), 0, length) for axis, length in enumerate(values.shape)]
        where[longest] = (where[longest] + shift) % values.shape[longest]
        spots.append(tuple(where))
    return values.at[spots[0]].set(low).at[spots[1]].set(high)


def block_scale(stream_key, dims, shards, smallest, largest):
    def one(dim, parts):
        steps = jax.random.uniform(jax.random.fold_in(jax.random.fold_in(stream_key, 6), dim), (parts,), jnp.float32, smallest / len(shards), largest / len(shards))
        return jnp.repeat(jnp.exp(steps), dims[dim] // parts).reshape((-1,) + (1,) * (len(dims) - dim - 1))

    gain = one(*shards[0])
    for cut in shards[1:]:
        gain = gain * one(*cut)
    return gain


def gaussian(own_key, dims, width, reach, pieces=(), kind=jnp.bfloat16):
    values = width * jax.random.normal(own_key, dims, jnp.float32)
    if pieces:
        values = values * block_scale(own_key, dims, pieces, -0.22, 0.18)
    return jnp.clip(values, -reach, reach).astype(kind)


def setup_inputs(seed: int = 0) -> dict:
    key_list = jax.random.split(jax.random.key(seed), 9)
    initial_replica_fields = gaussian(key_list[0], (WIN, REPLICA_TALLY, GRAPH_BLOCKS, BLOCK_CELLS), 1.0, 6.0, ((0, 2), (1, 4), (2, 32)), jnp.float32)
    sensor_jitter = gaussian(key_list[1], (WIN, CYCLES, REPLICA_TALLY, GRAPH_BLOCKS, BLOCK_CELLS), 1.0, 6.0, ((0, 2), (2, 4), (3, 32)), jnp.float32)
    measurements = gaussian(key_list[2], (WIN, CYCLES, GRAPH_BLOCKS, BLOCK_CELLS), 1.0, 6.0, ((0, 2), (2, 32)), jnp.float32)
    measured_indicator = set_ends((jax.random.randint(key_list[3], (WIN, CYCLES, GRAPH_BLOCKS, BLOCK_CELLS), 0, 2) < 1).astype(jnp.int32), jax.random.fold_in(key_list[3], 1), 0, 1)
    sensor_error_power = jnp.clip(jnp.exp(math.log(40960.0) - 2.3025851 * jax.random.uniform(key_list[4], (GRAPH_BLOCKS, BLOCK_CELLS), jnp.float32) ** block_scale(key_list[4], (GRAPH_BLOCKS, BLOCK_CELLS), ((0, 32),), -0.2, 0.2)), 4096.0, 40960.0)
    adjacent_tiles = draw_adjacent_tiles(jax.random.fold_in(key_list[8], 71), 0)
    coupling_operators = gaussian(key_list[6], (NEIGHBOUR_SLOTS, BLOCK_CELLS, BLOCK_CELLS), (NEIGHBOUR_SLOTS * BLOCK_CELLS) ** -0.5, 0.125)
    analysis_cotangent = gaussian(key_list[7], (WIN, REPLICA_TALLY, GRAPH_BLOCKS, BLOCK_CELLS), 1.0, 6.0, ((0, 2), (1, 4), (2, 32)), jnp.float32)
    return dict(initial_replica_fields=initial_replica_fields, sensor_jitter=sensor_jitter, measurements=measurements, measured_indicator=measured_indicator, sensor_error_power=sensor_error_power, adjacent_tiles=adjacent_tiles, coupling_operators=coupling_operators, analysis_cotangent=analysis_cotangent)


highest = lax.Precision.HIGHEST

def prediction_change(replica_fields, adjacent_tiles, coupling_operators):
    adjacent_line_tile = replica_fields.astype(jnp.bfloat16)[:, adjacent_tiles].reshape(-1, NEIGHBOUR_SLOTS * BLOCK_CELLS)
    amplifier_scalar = jnp.tanh(jnp.dot(adjacent_line_tile.astype(jnp.float32), coupling_operators.reshape(NEIGHBOUR_SLOTS * BLOCK_CELLS, BLOCK_CELLS).astype(jnp.float32), preferred_element_type=jnp.float32))
    amplifier_scalar = amplifier_scalar.reshape(replica_fields.shape)
    return (replica_fields + amplifier_scalar, adjacent_line_tile, amplifier_scalar)

def prediction_reverse(derivative_accumulated, adjacent_line_tile, amplifier_scalar, adjacent_tiles, coupling_operators):
    tanh_slope = (derivative_accumulated * (1.0 - amplifier_scalar * amplifier_scalar)).astype(jnp.bfloat16).reshape(-1, BLOCK_CELLS)
    weight_contribution = lax.dot_general(adjacent_line_tile.astype(jnp.float32), tanh_slope.astype(jnp.float32), (((0,), (0,)), ((), ())), preferred_element_type=jnp.float32)
    spread_backward = lax.dot_general(tanh_slope.astype(jnp.float32), coupling_operators.reshape(NEIGHBOUR_SLOTS * BLOCK_CELLS, BLOCK_CELLS).astype(jnp.float32), (((1,), (1,)), ((), ())), preferred_element_type=jnp.float32)
    spread_backward = spread_backward.reshape(derivative_accumulated.shape[0], GRAPH_BLOCKS, NEIGHBOUR_SLOTS, BLOCK_CELLS)
    shifted_states = jnp.zeros(derivative_accumulated.shape, jnp.float32).at[:, adjacent_tiles].add(spread_backward)
    return (derivative_accumulated + shifted_states, weight_contribution.reshape(NEIGHBOUR_SLOTS, BLOCK_CELLS, BLOCK_CELLS))

def assimilate_pass(predicted_field, jitter_replicas, measured_readings, indicator_line_tile, sensor_error_power):
    entire_horizon = predicted_field.reshape(REPLICA_TALLY, -1)
    member_spread = jnp.sqrt(jnp.float32(REPLICA_TALLY - 1))
    replica_departure_part = (entire_horizon - lax.optimization_barrier(jnp.mean(entire_horizon, axis=0))) / member_spread
    inverse_sd = 1.0 / jnp.sqrt(sensor_error_power.reshape(-1))
    mask_float = indicator_line_tile.reshape(-1).astype(jnp.float32)
    sensor_emphasis = mask_float * inverse_sd
    normalized_readings = sensor_emphasis * replica_departure_part
    misfit_array = mask_float * ((measured_readings.reshape(-1) - entire_horizon) * inverse_sd + jitter_replicas.reshape(REPLICA_TALLY, -1))
    gram = jnp.dot(normalized_readings, normalized_readings.T, precision=highest)
    joint_spread_product = jnp.dot(normalized_readings, misfit_array.T, precision=highest)
    identity_mat = jnp.eye(REPLICA_TALLY, dtype=jnp.float32)
    factor = jnp.linalg.cholesky(identity_mat + gram)
    reciprocal_operator = jax.scipy.linalg.cho_solve((factor, True), identity_mat)
    kalman_multiplier = jnp.dot(reciprocal_operator, joint_spread_product, precision=highest)
    corrected_field = entire_horizon + jnp.dot(kalman_multiplier.T, replica_departure_part, precision=highest)
    return (corrected_field.reshape(predicted_field.shape), (replica_departure_part, normalized_readings, misfit_array, sensor_emphasis, joint_spread_product, reciprocal_operator, kalman_multiplier))

def analyse_back(derivative_accumulated, stored):
    replica_departure_part, normalized_readings, misfit_array, sensor_emphasis, joint_spread_product, reciprocal_operator, kalman_multiplier = stored
    member_spread = jnp.sqrt(jnp.float32(REPLICA_TALLY - 1))
    flat_grad = derivative_accumulated.reshape(REPLICA_TALLY, -1)
    coeff_bar = jnp.dot(replica_departure_part, flat_grad.T, precision=highest)
    inverse_bar = jnp.dot(coeff_bar, joint_spread_product.T, precision=highest)
    cross_bar = jnp.dot(reciprocal_operator, coeff_bar, precision=highest)
    gram_bar = -jnp.dot(jnp.dot(reciprocal_operator, inverse_bar, precision=highest), reciprocal_operator, precision=highest)
    symmetric = gram_bar + gram_bar.T
    anomaly_bar = jnp.dot(kalman_multiplier, flat_grad, precision=highest)
    anomaly_bar = anomaly_bar + sensor_emphasis * (jnp.dot(symmetric, normalized_readings, precision=highest) + jnp.dot(cross_bar, misfit_array, precision=highest))
    innovation_bar = jnp.dot(cross_bar.T, normalized_readings, precision=highest)
    result = flat_grad + (anomaly_bar - lax.optimization_barrier(jnp.mean(anomaly_bar, axis=0))) / member_spread - sensor_emphasis * innovation_bar
    return result.reshape(derivative_accumulated.shape)

def reference(initial_replica_fields, sensor_jitter, measurements, measured_indicator, sensor_error_power, adjacent_tiles, coupling_operators, analysis_cotangent):
    summed_weight = jnp.zeros((NEIGHBOUR_SLOTS, BLOCK_CELLS, BLOCK_CELLS), jnp.float32)
    state_grads = []
    for horizon_period in range(WIN):
        initial_prediction, initial_lines, initial_amplifier = prediction_change(initial_replica_fields[horizon_period], adjacent_tiles, coupling_operators)
        initial_corrected, initial_retained = assimilate_pass(initial_prediction, sensor_jitter[horizon_period, 0], measurements[horizon_period, 0], measured_indicator[horizon_period, 0], sensor_error_power)
        later_prediction, later_lines, later_amplifier = prediction_change(initial_corrected, adjacent_tiles, coupling_operators)
        later_corrected, later_retained = assimilate_pass(later_prediction, sensor_jitter[horizon_period, 1], measurements[horizon_period, 1], measured_indicator[horizon_period, 1], sensor_error_power)
        derivative_accumulated = analyse_back(analysis_cotangent[horizon_period], later_retained)
        derivative_accumulated, trailing_summand = prediction_reverse(derivative_accumulated, later_lines, later_amplifier, adjacent_tiles, coupling_operators)
        derivative_accumulated = analyse_back(derivative_accumulated, initial_retained)
        derivative_accumulated, leading_summand = prediction_reverse(derivative_accumulated, initial_lines, initial_amplifier, adjacent_tiles, coupling_operators)
        summed_weight = summed_weight + leading_summand + trailing_summand
        state_grads.append(derivative_accumulated)
    weight_grad = summed_weight / jnp.sqrt(jnp.float32(WIN * REPLICA_TALLY * GRAPH_BLOCKS))
    return (weight_grad, jnp.stack(state_grads))
```

```python
import math

import jax
import jax.numpy as jnp
from jax import lax
from jax.experimental import pallas as pl
from jax.experimental.pallas import tpu as pltpu
from jax.sharding import PartitionSpec as P

R = 2
INTERPRET = False
F32 = jnp.float32
BF16 = jnp.bfloat16
HI = lax.Precision.HIGHEST
VM = pl.BlockSpec(memory_space=pltpu.VMEM)
SM = pl.BlockSpec(memory_space=pltpu.SMEM)


def nn(a, b):
    return lax.dot_general(a, b, (((1,), (0,)), ((), ())), precision=HI, preferred_element_type=F32)


def nt(a, b):
    return lax.dot_general(a, b, (((1,), (1,)), ((), ())), precision=HI, preferred_element_type=F32)


def call(body, outs, scratch, *args):
    return pl.pallas_call(
        body,
        out_shape=[jax.ShapeDtypeStruct(s, d) for s, d in outs],
        in_specs=[SM if kind == "S" else VM for kind, _ in args],
        out_specs=[VM] * len(outs),
        scratch_shapes=[pltpu.VMEM(s, d) for s, d in scratch],
        interpret=INTERPRET,
    )(*[a for _, a in args])


def spd_inverse(a):
    n = a.shape[0]
    row_ids = lax.broadcasted_iota(jnp.int32, (n, n), 0)
    col_ids = lax.broadcasted_iota(jnp.int32, (n, n), 1)
    for k in range(n):
        row = jnp.broadcast_to(a[k : k + 1, :], (n, n))
        col = jnp.broadcast_to(a[:, k : k + 1], (n, n))
        inv = 1.0 / jnp.broadcast_to(a[k : k + 1, k : k + 1], (n, n))
        on_row, on_col = row_ids == k, col_ids == k
        scaled = row * inv
        a = jnp.where(
            on_row,
            jnp.where(on_col, -inv, scaled),
            jnp.where(on_col, col * inv, a - col * scaled),
        )
    return -a


def local(
    initial_replica_fields,
    sensor_jitter,
    measurements,
    measured_indicator,
    sensor_error_power,
    adjacent_tiles,
    coupling_operators,
    analysis_cotangent,
):
    K, C = coupling_operators.shape[0], coupling_operators.shape[1]
    m_own, b_own = initial_replica_fields.shape[1], initial_replica_fields.shape[2]
    spaces, groups, windows = (lax.axis_size(a) for a in ("space", "member", "window"))
    N = m_own * groups
    NB = b_own // groups
    total = b_own * spaces
    spread = math.sqrt(N - 1.0)
    y = lax.axis_index("member").astype(jnp.int32)
    s = lax.axis_index("space").astype(jnp.int32)
    pos = jnp.stack([s, y])
    weights = coupling_operators.reshape(K * C, C)
    field = (NB, N, C)
    piece = (NB, m_own, C)
    half = (R, N, C)

    def swap_member(a, d):
        return lax.ppermute(a, "member", [(i, i ^ d) for i in range(groups)])

    def swap_space(a, d):
        return lax.ppermute(a, "space", [(i, i ^ d) for i in range(spaces)])

    def swap_window(a):
        return lax.ppermute(a, "window", [(i, i ^ 1) for i in range(windows)])

    chain = spaces * groups

    def to_next(a):
        return lax.ppermute(a, ("space", "member"), [(i, (i + 1) % chain) for i in range(chain)])

    def to_prev(a):
        return lax.ppermute(a, ("space", "member"), [(i, (i - 1) % chain) for i in range(chain)])

    def sum_all(a):
        for d in (1, 3):
            a = a + swap_member(a, d)
        for d in (1, 2, 6, 8, 24):
            a = a + swap_space(a, d)
        return a

    def pack(x, dtype):
        def body(pos_ref, x_ref, o0, o1, o2, o3, t_ref):
            for b in range(b_own):
                t_ref[b] = x_ref[:, b, :].astype(dtype)
            for d, o in enumerate((o0, o1, o2, o3)):
                o[...] = t_ref[pl.ds(NB * (pos_ref[1] ^ d), NB)]

        pieces = call(
            body, [(piece, dtype)] * 4, [((b_own, m_own, C), dtype)], ("S", pos), ("V", x)
        )
        return [pieces[0]] + [swap_member(pieces[d], d) for d in (1, 2, 3)]

    def merged(pos_ref, refs, t_ref):
        for d, r in enumerate(refs):
            t_ref[pos_ref[1] ^ d] = r[...]
        return lambda b: t_ref[:, b].reshape(N, C)

    prior_pieces = pack(initial_replica_fields[0], F32)
    jitter_pieces = [pack(sensor_jitter[0, c], BF16) for c in (0, 1)]
    cotangent_pieces = pack(analysis_cotangent[0], F32)
    stack4 = (groups,) + piece

    def merge_body(pos_ref, p0, p1, p2, p3, f_ref, lo_ref, hi_ref, t_ref):
        block = merged(pos_ref, (p0, p1, p2, p3), t_ref)
        for b in range(NB):
            v = block(b)
            f_ref[b] = v
            (lo_ref if b < R else hi_ref)[b % R] = v.astype(BF16)

    prior_1, lo, hi = call(
        merge_body,
        [(field, F32), (half, BF16), (half, BF16)],
        [(stack4, F32)],
        ("S", pos),
        *[("V", p) for p in prior_pieces],
    )

    def slot(pos_ref, adj_ref, b, k):
        b_here = NB * pos_ref[1] + b
        own = b_own * pos_ref[0] + b_here
        off = lax.rem(adj_ref[b_here, k] - own + total + total // 2, total) - total // 2
        return b + R + off

    def obs(pos_ref, mask_ref, err_ref, c, b):
        at = NB * pos_ref[1] + b
        mask = mask_ref[c, pl.ds(at, 1), :].astype(F32)
        inv_sd = 1.0 / jnp.sqrt(err_ref[pl.ds(at, 1), :])
        return mask, inv_sd

    def forward(c, prior, lo, hi):
        from_prev, from_next = to_next(hi), to_prev(lo)
        last = c == 1

        def body(*refs):
            (pos_ref, adj_ref, prev_ref, next_ref, prior_ref, w_ref, meas_ref, mask_ref, err_ref) = refs[:9]
            refs = refs[9:]
            jit, refs = refs[:4], refs[4:]
            if last:
                cot, refs = refs[:4], refs[4:]
                rows_ref, grow_ref, fc_ref, an_ref, inn_ref, gc_ref, g_ref, pad_ref, j_ref, c_ref = refs
                g_block = merged(pos_ref, cot, c_ref)
            else:
                rows_ref, grow_ref, fc_ref, an_ref, inn_ref, gc_ref, pad_ref, j_ref = refs
            j_block = merged(pos_ref, jit, j_ref)
            pad_ref[0:R] = prev_ref[...]
            pad_ref[R : R + NB] = prior_ref[...].astype(BF16)
            pad_ref[R + NB :] = next_ref[...]
            acc = jnp.zeros((NB * N, C), F32)
            for k in range(K):
                for b in range(NB):
                    rows_ref[k, b * N : (b + 1) * N, :] = pad_ref[slot(pos_ref, adj_ref, b, k)]
                acc = acc + jnp.dot(
                    rows_ref[k], w_ref[k * C : (k + 1) * C, :], preferred_element_type=F32
                )
            growth = jnp.tanh(acc)
            gram = jnp.zeros((N, N), F32)
            cross = jnp.zeros((N, N), F32)
            cbar = jnp.zeros((N, N), F32)
            for b in range(NB):
                grow = growth[b * N : (b + 1) * N]
                fc = prior_ref[b] + grow
                an = (fc - jnp.mean(fc, axis=0, keepdims=True)) / spread
                mask, inv_sd = obs(pos_ref, mask_ref, err_ref, c, b)
                sc = (mask * inv_sd) * an
                meas = meas_ref[c, pl.ds(NB * pos_ref[1] + b, 1), :]
                inn = mask * ((meas - fc) * inv_sd + j_block(b).astype(F32))
                grow_ref[b] = grow
                fc_ref[b] = fc
                an_ref[b] = an
                inn_ref[b] = inn
                gram = gram + nt(sc, sc)
                cross = cross + nt(sc, inn)
                if last:
                    g = g_block(b)
                    g_ref[b] = g
                    cbar = cbar + nt(an, g)
            gc_ref[0] = gram
            gc_ref[1] = cross
            if last:
                gc_ref[2] = cbar

        mats = 3 if last else 2
        outs = [((K, NB * N, C), BF16)] + [(field, F32)] * 4 + [((mats, N, N), F32)]
        scratch = [((NB + 2 * R, N, C), BF16), (stack4, BF16)]
        args = [
            ("S", pos), ("S", adjacent_tiles), ("V", from_prev), ("V", from_next), ("V", prior),
            ("V", weights), ("V", measurements[0]), ("V", measured_indicator[0]),
            ("V", sensor_error_power),
        ] + [("V", p) for p in jitter_pieces[c]]
        if last:
            outs.append((field, F32))
            scratch.append((stack4, F32))
            args += [("V", p) for p in cotangent_pieces]
        return call(body, outs, scratch, *args)

    def solve(gc_ref):
        ident = (
            lax.broadcasted_iota(jnp.int32, (N, N), 0) == lax.broadcasted_iota(jnp.int32, (N, N), 1)
        ).astype(F32)
        inverse = spd_inverse(ident + gc_ref[0])
        return inverse, nn(inverse, gc_ref[1])

    def analysis_body(gc_ref, fc_ref, an_ref, inv_ref, co_ref, a_ref, lo_ref, hi_ref):
        inverse, coeff = solve(gc_ref)
        inv_ref[...] = inverse
        co_ref[...] = coeff
        coeff_t = coeff.T
        for b in range(NB):
            v = fc_ref[b] + nn(coeff_t, an_ref[b])
            a_ref[b] = v
            (lo_ref if b < R else hi_ref)[b % R] = v.astype(BF16)

    def backward(c, pos_ref, adj_ref, mask_ref, err_ref, w_ref, inverse, coeff, cbar, an_ref, inn_ref,
                 g_ref, grow_ref, slope_ref, own_ref, lo_ref, hi_ref, acc_ref):
        cross_bar = nn(inverse, cbar)
        gram_bar = -nt(cross_bar, coeff)
        sym = gram_bar + gram_bar.T

        def centered(m):
            return (m - jnp.mean(m, axis=0, keepdims=True)) / spread

        on_scaled = centered(sym) - cross_bar.T
        on_inn = centered(cross_bar)
        on_g = centered(coeff)
        acc_ref[...] = jnp.zeros(acc_ref.shape, F32)
        for b in range(NB):
            mask, inv_sd = obs(pos_ref, mask_ref, err_ref, c, b)
            weight = mask * inv_sd
            g = g_ref[b]
            fbar = g + nn(on_g, g) + weight * (
                nn(on_scaled, weight * an_ref[b]) + nn(on_inn, inn_ref[b])
            )
            grow = grow_ref[b]
            slope_ref[b * N : (b + 1) * N, :] = (fbar * (1.0 - grow * grow)).astype(BF16)
            acc_ref[R + b] = fbar
        for k in range(K):
            back = lax.dot_general(
                slope_ref[...], w_ref[k * C : (k + 1) * C, :], (((1,), (1,)), ((), ())),
                preferred_element_type=F32,
            )
            for b in range(NB):
                at = slot(pos_ref, adj_ref, b, k)
                acc_ref[at] = acc_ref[at] + back[b * N : (b + 1) * N]
        lo_ref[...] = acc_ref[0:R]
        own_ref[...] = acc_ref[R : R + NB]
        hi_ref[...] = acc_ref[R + NB :]

    back_outs = [((NB * N, C), BF16), (field, F32), (half, F32), (half, F32)]
    back_scratch = [((NB + 2 * R, N, C), F32)]

    def back_2_body(pos_ref, adj_ref, mask_ref, err_ref, w_ref, gc_ref, an_ref, inn_ref, g_ref, grow_ref,
                    slope_ref, own_ref, lo_ref, hi_ref, acc_ref):
        inverse, coeff = solve(gc_ref)
        backward(1, pos_ref, adj_ref, mask_ref, err_ref, w_ref, inverse, coeff, gc_ref[2], an_ref,
                 inn_ref, g_ref, grow_ref, slope_ref, own_ref, lo_ref, hi_ref, acc_ref)

    def back_1_body(pos_ref, adj_ref, mask_ref, err_ref, w_ref, inv_ref, co_ref, cb_ref, an_ref, inn_ref,
                    g_ref, grow_ref, slope_ref, own_ref, lo_ref, hi_ref, acc_ref):
        backward(0, pos_ref, adj_ref, mask_ref, err_ref, w_ref, inv_ref[...], co_ref[...], cb_ref[...],
                 an_ref, inn_ref, g_ref, grow_ref, slope_ref, own_ref, lo_ref, hi_ref, acc_ref)

    def receive_body(own_ref, first_ref, last_ref, an_ref, g_ref, cb_ref):
        cbar = jnp.zeros((N, N), F32)
        for b in range(NB):
            g = own_ref[b] + (first_ref[b] if b < R else last_ref[b - (NB - R)])
            g_ref[b] = g
            cbar = cbar + nt(an_ref[b], g)
        cb_ref[...] = cbar

    statics = [("S", pos), ("S", adjacent_tiles), ("V", measured_indicator[0]), ("V", sensor_error_power),
               ("V", weights)]

    rows_1, grow_1, fc_1, an_1, inn_1, gc_1 = forward(0, prior_1, lo, hi)
    gc_1 = sum_all(gc_1)
    inv_1, co_1, prior_2, lo, hi = call(
        analysis_body,
        [((N, N), F32), ((N, N), F32), (field, F32), (half, BF16), (half, BF16)],
        [],
        ("V", gc_1), ("V", fc_1), ("V", an_1),
    )
    rows_2, grow_2, _, an_2, inn_2, gc_2, g_2 = forward(1, prior_2, lo, hi)
    gc_2 = sum_all(gc_2)
    slope_2, own, lo, hi = call(
        back_2_body, back_outs, back_scratch, *statics,
        ("V", gc_2), ("V", an_2), ("V", inn_2), ("V", g_2), ("V", grow_2),
    )
    g_1, cb_1 = call(
        receive_body, [(field, F32), ((N, N), F32)], [],
        ("V", own), ("V", to_next(hi)), ("V", to_prev(lo)), ("V", an_1),
    )
    cb_1 = sum_all(cb_1)
    slope_1, own, lo, hi = call(
        back_1_body, back_outs, back_scratch, *statics,
        ("V", inv_1), ("V", co_1), ("V", cb_1), ("V", an_1), ("V", inn_1), ("V", g_1), ("V", grow_1),
    )

    X, Z = 4, 4
    rows_each = C // spaces
    hc = C // 2
    keep_shape = (4, 4, Z, rows_each, hc)
    scale = 1.0 / math.sqrt(windows * N * total)

    def weight_body(pos_ref, r1_ref, s1_ref, r2_ref, s2_ref, k0_ref, k1_ref, t0_ref, t1_ref, p_ref):
        at = pos_ref[0]
        own_x, own_z, own_c = at // 8, (at // 2) % 4, at % 2
        tn = (((0,), (0,)), ((), ()))
        for yr in range(groups):
            k = yr ^ pos_ref[1]
            p_ref[...] = (
                lax.dot_general(r1_ref[k], s1_ref[...], tn, preferred_element_type=F32)
                + lax.dot_general(r2_ref[k], s2_ref[...], tn, preferred_element_type=F32)
            ) * scale
            for xr in range(X):
                for zr in range(Z):
                    base = (own_x ^ xr) * 8 + (own_z ^ zr) * 2
                    mine = p_ref[pl.ds((base + own_c) * rows_each, rows_each), :]
                    k0_ref[yr, xr, zr] = mine[:, :hc]
                    k1_ref[xr, yr, zr] = mine[:, hc:]
                    other = p_ref[pl.ds((base + (own_c ^ 1)) * rows_each, rows_each), :].astype(BF16)
                    t0_ref[yr, xr, zr] = other[:, :hc]
                    t1_ref[xr, yr, zr] = other[:, hc:]

    keep_y, keep_x, give_y, give_x = call(
        weight_body,
        [(keep_shape, F32), (keep_shape, F32), (keep_shape, BF16), (keep_shape, BF16)],
        [((C, C), F32)],
        ("S", pos), ("V", rows_1), ("V", slope_1), ("V", rows_2), ("V", slope_2),
    )
    part_y = keep_y + swap_space(give_y, 1).astype(F32)
    part_x = keep_x + swap_space(give_x, 1).astype(F32)

    def halve(a, swap, unit, dtype):
        got = swap(a[1:3].astype(dtype), unit).astype(F32)
        rest = swap((a[3] + got[1]).astype(dtype), 3 * unit).astype(F32)
        return (a[0] + got[0]) + rest

    part_y = halve(part_y, swap_member, 1, BF16)
    part_x = halve(part_x, swap_space, 8, BF16)
    part_y = halve(part_y, swap_space, 8, F32)
    part_x = halve(part_x, swap_member, 1, F32)
    part = halve(jnp.concatenate([part_y, part_x], axis=-1), swap_space, 2, F32)
    part = part + swap_window(part)
    near = swap_member(part, 1)
    pair = jnp.stack([part, near])
    far = swap_member(pair, 3)

    def unpack_body(pos_ref, own_ref, first_ref, last_ref, o0, o1, o2, o3, t_ref):
        for b in range(NB):
            t_ref[b] = own_ref[b] + (first_ref[b] if b < R else last_ref[b - (NB - R)])
        for d, o in enumerate((o0, o1, o2, o3)):
            start = pl.multiple_of(m_own * (pos_ref[1] ^ d), m_own)
            for b in range(NB):
                o[b] = t_ref[b, pl.ds(start, m_own), :]

    pieces = call(
        unpack_body, [(piece, F32)] * 4, [(field, F32)],
        ("S", pos), ("V", own), ("V", to_next(hi)), ("V", to_prev(lo)),
    )
    pieces = [pieces[0]] + [swap_member(pieces[d], d) for d in (1, 2, 3)]

    def finish_body(pos_ref, p0, p1, p2, p3, o_ref, t_ref):
        for d, r in enumerate((p0, p1, p2, p3)):
            t_ref[pl.ds(NB * (pos_ref[1] ^ d), NB)] = r[...]
        for b in range(b_own):
            o_ref[:, b, :] = t_ref[b]

    (grad,) = call(
        finish_body, [((m_own, b_own, C), F32)], [((b_own, m_own, C), F32)],
        ("S", pos), *[("V", p) for p in pieces],
    )

    def rows_body(pos_ref, a_ref, f_ref, o_ref):
        o_ref[pos_ref[1]] = a_ref[0]
        o_ref[pos_ref[1] ^ 1] = a_ref[1]
        o_ref[pos_ref[1] ^ 3] = f_ref[0]
        o_ref[pos_ref[1] ^ 2] = f_ref[1]

    (weight_grad,) = call(
        rows_body, [((K, rows_each, C), F32)], [], ("S", pos), ("V", pair), ("V", far)
    )
    return weight_grad, grad[None]


def solution(mesh):
    in_specs = (
        P("window", "member", "space", None),
        P("window", None, "member", "space", None),
        P("window", None, "space", None),
        P("window", None, "space", None),
        P("space", None),
        P("space", None),
        P(),
        P("window", "member", "space", None),
    )
    out_specs = (P(None, "space", None), P("window", "member", "space", None))
    return jax.shard_map(local, mesh=mesh, in_specs=in_specs, out_specs=out_specs, check_vma=False)
```

```python
import math

import jax
import jax.numpy as jnp
from jax import lax
from jax.experimental import pallas as pl
from jax.experimental.pallas import tpu as pltpu
from jax.sharding import PartitionSpec as P

R = 2
INTERPRET = False
F32 = jnp.float32
BF16 = jnp.bfloat16
HI = lax.Precision.HIGHEST
VM = pl.BlockSpec(memory_space=pltpu.VMEM)
SM = pl.BlockSpec(memory_space=pltpu.SMEM)


def nn(a, b):
    return lax.dot_general(a, b, (((1,), (0,)), ((), ())), precision=HI, preferred_element_type=F32)


def nt(a, b):
    return lax.dot_general(a, b, (((1,), (1,)), ((), ())), precision=HI, preferred_element_type=F32)


def call(body, outs, scratch, *args):
    specs = {"S": SM, "V": VM}
    windowed = any(not isinstance(kind, str) for kind, _ in args)
    return pl.pallas_call(
        body,
        grid=(1,) if windowed else (),
        out_shape=[jax.ShapeDtypeStruct(s, d) for s, d in outs],
        in_specs=[specs[kind] if isinstance(kind, str) else kind for kind, _ in args],
        out_specs=[VM] * len(outs),
        scratch_shapes=[pltpu.VMEM(s, d) for s, d in scratch],
        interpret=INTERPRET,
    )(*[a for _, a in args])


def small_inverse(m):
    n = len(m)
    if n == 1:
        return [[1.0 / m[0][0]]]
    h = n // 2
    top = small_inverse([r[:h] for r in m[:h]])
    c = [r[:h] for r in m[h:]]
    ct = [[sum(c[i][p] * top[p][j] for p in range(h)) for j in range(h)] for i in range(h)]
    schur = [
        [m[h + i][h + j] - sum(ct[i][p] * c[j][p] for p in range(h)) for j in range(h)]
        for i in range(h)
    ]
    low = small_inverse(schur)
    cross = [[-sum(low[i][p] * ct[p][j] for p in range(h)) for j in range(h)] for i in range(h)]
    first = [
        [top[i][j] - sum(ct[p][i] * cross[p][j] for p in range(h)) for j in range(h)] for i in range(h)
    ]
    return [first[i] + [cross[p][i] for p in range(h)] for i in range(h)] + [
        cross[i] + low[i] for i in range(h)
    ]


def spd_inverse(a, step=4):
    n = a.shape[0]
    row_ids = lax.broadcasted_iota(jnp.int32, (n, n), 0)
    col_ids = lax.broadcasted_iota(jnp.int32, (n, n), 1)
    lane = lax.broadcasted_iota(jnp.int32, (1, n), 1)
    for k in range(0, n, step):
        at = range(k, k + step)
        cols = [jnp.broadcast_to(a[:, q : q + 1], (n, n)) for q in at]
        rows = [a[q : q + 1, :] for q in at]
        inv = small_inverse([[cols[q][p : p + 1, :] for q in range(step)] for p in at])
        a = jnp.where(col_ids // step == k // step, 0.0, a)
        for q in range(step):
            new = sum(inv[q][p] * rows[p] for p in range(step))
            for p in range(step):
                new = jnp.where(lane == k + p, -inv[q][p], new)
            new = jnp.broadcast_to(new, (n, n))
            a = a - cols[q] * new
            cols[q] = new
        for q in range(step):
            a = jnp.where(row_ids == k + q, cols[q], a)
    return -a


def local(
    initial_replica_fields,
    sensor_jitter,
    measurements,
    measured_indicator,
    sensor_error_power,
    adjacent_tiles,
    coupling_operators,
    analysis_cotangent,
):
    K, C = coupling_operators.shape[0], coupling_operators.shape[1]
    m_own, b_own = initial_replica_fields.shape[1], initial_replica_fields.shape[2]
    spaces, groups, windows = (lax.axis_size(a) for a in ("space", "member", "window"))
    N = m_own * groups
    NB = b_own // groups
    total = b_own * spaces
    spread = math.sqrt(N - 1.0)
    y = lax.axis_index("member").astype(jnp.int32)
    s = lax.axis_index("space").astype(jnp.int32)
    turn = groups - 1
    q = y ^ (turn * (s % 2))
    pos = jnp.stack([s, y, q])
    weights = coupling_operators.reshape(K * C, C)
    field = (NB, N, C)
    piece = (NB, m_own, C)
    half = (R, N, C)
    triple = (NB, 3, m_own, C)

    def swap_member(a, d):
        return lax.ppermute(a, "member", [(i, i ^ d) for i in range(groups)])

    def swap_space(a, d):
        return lax.ppermute(a, "space", [(i, i ^ d) for i in range(spaces)])

    def swap_window(a):
        return lax.ppermute(a, "window", [(i, i ^ 1) for i in range(windows)])

    order = [i * groups + (j ^ (turn * (i % 2))) for i in range(spaces) for j in range(groups)]
    ahead = order[1:] + order[:1]

    def to_next(a):
        return lax.ppermute(a, ("space", "member"), list(zip(order, ahead)))

    def to_prev(a):
        return lax.ppermute(a, ("space", "member"), list(zip(ahead, order)))

    def sum_all(a):
        for d in (1, 3):
            a = a + swap_member(a, d)
        for d in (1, 2, 6, 8, 24):
            a = a + swap_space(a, d)
        return a

    def pack(x, c):
        def body(pos_ref, x_ref, j_ref, o0, o1, o2, o3, t_ref):
            for b in range(b_own):
                v = x_ref[:, b, :]
                high = v.astype(BF16)
                t_ref[b, 0] = high
                t_ref[b, 1] = (v - high.astype(F32)).astype(BF16)
                t_ref[b, 2] = j_ref[0, :, b, :].astype(BF16)
            for d, o in enumerate((o0, o1, o2, o3)):
                o[...] = t_ref[pl.ds(NB * (pos_ref[2] ^ d), NB)]

        one_cycle = pl.BlockSpec((1, m_own, b_own, C), lambda i: (c, 0, 0, 0))
        pieces = call(
            body, [(triple, BF16)] * 4, [((b_own, 3, m_own, C), BF16)],
            ("S", pos), ("V", x), (one_cycle, sensor_jitter[0]),
        )
        return [pieces[0]] + [swap_member(pieces[d], d) for d in (1, 2, 3)]

    def merge(pieces, halos):
        def body(pos_ref, p0, p1, p2, p3, f_ref, j_ref, *rest):
            t_ref = rest[-1]
            for d, r in enumerate((p0, p1, p2, p3)):
                t_ref[pos_ref[1] ^ d] = r[...]
            for b in range(NB):
                high = t_ref[:, b, 0].reshape(N, C)
                f_ref[b] = high.astype(F32) + t_ref[:, b, 1].reshape(N, C).astype(F32)
                j_ref[b] = t_ref[:, b, 2].reshape(N, C)
                if halos:
                    rest[0 if b < R else 1][b % R] = high

        outs = [(field, F32), (field, BF16)] + ([(half, BF16)] * 2 if halos else [])
        return call(body, outs, [((groups,) + triple, BF16)], ("S", pos), *[("V", p) for p in pieces])

    prior_1, jitter_1, lo, hi = merge(pack(initial_replica_fields[0], 0), True)
    g_2, jitter_2 = merge(pack(analysis_cotangent[0], 1), False)

    def fold(m):
        return jnp.concatenate([m[: N // 2], m[N // 2 :]], axis=1)

    def unfold(m):
        return jnp.concatenate([m[:, :N], m[:, N:]], axis=0)

    def slot(pos_ref, adj_ref, b, k):
        b_here = NB * pos_ref[2] + b
        own = b_own * pos_ref[0] + b_here
        off = lax.rem(adj_ref[b_here, k] - own + total + total // 2, total) - total // 2
        return b + R + off

    def obs(pos_ref, mask_ref, err_ref, c, b):
        at = NB * pos_ref[2] + b
        mask = mask_ref[c, pl.ds(at, 1), :].astype(F32)
        inv_sd = 1.0 / jnp.sqrt(err_ref[pl.ds(at, 1), :])
        return mask, inv_sd

    def forward(c, prior, jitter, lo, hi):
        from_prev, from_next = to_next(hi), to_prev(lo)
        last = c == 1

        def body(*refs):
            (pos_ref, adj_ref, prev_ref, next_ref, prior_ref, w_ref, meas_ref, mask_ref, err_ref) = refs[:9]
            j_ref, refs = refs[9], refs[10:]
            if last:
                g_ref, refs = refs[0], refs[1:]
            rows_ref, grow_ref, fc_ref, an_ref, inn_ref, gc_ref, pad_ref = refs
            pad_ref[0:R] = prev_ref[...]
            pad_ref[R : R + NB] = prior_ref[...].astype(BF16)
            pad_ref[R + NB :] = next_ref[...]
            acc = jnp.zeros((NB * N, C), F32)
            for k in range(K):
                for b in range(NB):
                    rows_ref[k, b * N : (b + 1) * N, :] = pad_ref[slot(pos_ref, adj_ref, b, k)]
                acc = acc + jnp.dot(
                    rows_ref[k], w_ref[k * C : (k + 1) * C, :], preferred_element_type=F32
                )
            growth = jnp.tanh(acc)
            sums = jnp.zeros((N, 2 * N), F32)
            cbar = jnp.zeros((N, N), F32)
            for b in range(NB):
                grow = growth[b * N : (b + 1) * N]
                fc = prior_ref[b] + grow
                an = (fc - jnp.mean(fc, axis=0, keepdims=True)) / spread
                mask, inv_sd = obs(pos_ref, mask_ref, err_ref, c, b)
                sc = (mask * inv_sd) * an
                meas = meas_ref[c, pl.ds(NB * pos_ref[2] + b, 1), :]
                inn = mask * ((meas - fc) * inv_sd + j_ref[b].astype(F32))
                grow_ref[b] = grow
                fc_ref[b] = fc
                an_ref[b] = an
                inn_ref[b] = inn
                sums = sums + nt(sc, jnp.concatenate([sc, inn], axis=0))
                if last:
                    cbar = cbar + nt(an, g_ref[b])
            gc_ref[0:N] = sums
            if last:
                gc_ref[N:] = fold(cbar)

        outs = [((K, NB * N, C), BF16)] + [(field, F32)] * 4
        outs.append((((3 * N // 2 if last else N), 2 * N), F32))
        scratch = [((NB + 2 * R, N, C), BF16)]
        args = [
            ("S", pos), ("S", adjacent_tiles), ("V", from_prev), ("V", from_next), ("V", prior),
            ("V", weights), ("V", measurements[0]), ("V", measured_indicator[0]),
            ("V", sensor_error_power), ("V", jitter),
        ]
        if last:
            args.append(("V", g_2))
        return call(body, outs, scratch, *args)

    def solve(gc_ref):
        ident = (
            lax.broadcasted_iota(jnp.int32, (N, N), 0) == lax.broadcasted_iota(jnp.int32, (N, N), 1)
        ).astype(F32)
        inverse = spd_inverse(ident + gc_ref[0:N, 0:N])
        return inverse, nn(inverse, gc_ref[0:N, N:])

    def analysis_body(gc_ref, fc_ref, an_ref, inv_ref, co_ref, a_ref, lo_ref, hi_ref):
        inverse, coeff = solve(gc_ref)
        inv_ref[...] = inverse
        co_ref[...] = coeff
        coeff_t = coeff.T
        for b in range(NB):
            v = fc_ref[b] + nn(coeff_t, an_ref[b])
            a_ref[b] = v
            (lo_ref if b < R else hi_ref)[b % R] = v.astype(BF16)

    def backward(c, pos_ref, adj_ref, mask_ref, err_ref, w_ref, inverse, coeff, cbar, an_ref, inn_ref,
                 g_ref, grow_ref, slope_ref, own_ref, lo_ref, hi_ref, acc_ref):
        cross_bar = nn(inverse, cbar)
        gram_bar = -nt(cross_bar, coeff)
        sym = gram_bar + gram_bar.T

        def centered(m):
            return (m - jnp.mean(m, axis=0, keepdims=True)) / spread

        on_scaled = centered(sym) - cross_bar.T
        on_inn = centered(cross_bar)
        on_g = centered(coeff)
        acc_ref[...] = jnp.zeros(acc_ref.shape, F32)
        for b in range(NB):
            mask, inv_sd = obs(pos_ref, mask_ref, err_ref, c, b)
            weight = mask * inv_sd
            g = g_ref[b]
            fbar = g + nn(on_g, g) + weight * (
                nn(on_scaled, weight * an_ref[b]) + nn(on_inn, inn_ref[b])
            )
            grow = grow_ref[b]
            slope_ref[b * N : (b + 1) * N, :] = (fbar * (1.0 - grow * grow)).astype(BF16)
            acc_ref[R + b] = fbar
        for k in range(K):
            back = lax.dot_general(
                slope_ref[...], w_ref[k * C : (k + 1) * C, :], (((1,), (1,)), ((), ())),
                preferred_element_type=F32,
            )
            for b in range(NB):
                at = slot(pos_ref, adj_ref, b, k)
                acc_ref[at] = acc_ref[at] + back[b * N : (b + 1) * N]
        lo_ref[...] = acc_ref[0:R]
        own_ref[...] = acc_ref[R : R + NB]
        hi_ref[...] = acc_ref[R + NB :]

    back_outs = [((NB * N, C), BF16), (field, F32), (half, F32), (half, F32)]
    back_scratch = [((NB + 2 * R, N, C), F32)]

    def back_2_body(pos_ref, adj_ref, mask_ref, err_ref, w_ref, gc_ref, an_ref, inn_ref, g_ref, grow_ref,
                    slope_ref, own_ref, lo_ref, hi_ref, acc_ref):
        inverse, coeff = solve(gc_ref)
        backward(1, pos_ref, adj_ref, mask_ref, err_ref, w_ref, inverse, coeff, unfold(gc_ref[N:]), an_ref,
                 inn_ref, g_ref, grow_ref, slope_ref, own_ref, lo_ref, hi_ref, acc_ref)

    def back_1_body(pos_ref, adj_ref, mask_ref, err_ref, w_ref, inv_ref, co_ref, cb_ref, an_ref, inn_ref,
                    g_ref, grow_ref, slope_ref, own_ref, lo_ref, hi_ref, acc_ref):
        backward(0, pos_ref, adj_ref, mask_ref, err_ref, w_ref, inv_ref[...], co_ref[...], unfold(cb_ref[...]),
                 an_ref, inn_ref, g_ref, grow_ref, slope_ref, own_ref, lo_ref, hi_ref, acc_ref)

    def receive_body(own_ref, first_ref, last_ref, an_ref, g_ref, cb_ref):
        cbar = jnp.zeros((N, N), F32)
        for b in range(NB):
            g = own_ref[b] + (first_ref[b] if b < R else last_ref[b - (NB - R)])
            g_ref[b] = g
            cbar = cbar + nt(an_ref[b], g)
        cb_ref[...] = fold(cbar)

    statics = [("S", pos), ("S", adjacent_tiles), ("V", measured_indicator[0]), ("V", sensor_error_power),
               ("V", weights)]

    rows_1, grow_1, fc_1, an_1, inn_1, gc_1 = forward(0, prior_1, jitter_1, lo, hi)
    gc_1 = sum_all(gc_1)
    inv_1, co_1, prior_2, lo, hi = call(
        analysis_body,
        [((N, N), F32), ((N, N), F32), (field, F32), (half, BF16), (half, BF16)],
        [],
        ("V", gc_1), ("V", fc_1), ("V", an_1),
    )
    rows_2, grow_2, _, an_2, inn_2, gc_2 = forward(1, prior_2, jitter_2, lo, hi)
    gc_2 = sum_all(gc_2)
    slope_2, own, lo, hi = call(
        back_2_body, back_outs, back_scratch, *statics,
        ("V", gc_2), ("V", an_2), ("V", inn_2), ("V", g_2), ("V", grow_2),
    )
    g_1, cb_1 = call(
        receive_body, [(field, F32), ((N // 2, 2 * N), F32)], [],
        ("V", own), ("V", to_next(hi)), ("V", to_prev(lo)), ("V", an_1),
    )
    cb_1 = sum_all(cb_1)
    slope_1, own, lo, hi = call(
        back_1_body, back_outs, back_scratch, *statics,
        ("V", inv_1), ("V", co_1), ("V", cb_1), ("V", an_1), ("V", inn_1), ("V", g_1), ("V", grow_1),
    )

    X, Z = 4, 4
    rows_each = C // spaces
    hc = C // 2
    keep_shape = (4, 4, Z, rows_each, hc)
    scale = 1.0 / math.sqrt(windows * N * total)

    def weight_body(pos_ref, r1_ref, s1_ref, r2_ref, s2_ref, k0_ref, k1_ref, t0_ref, t1_ref, p_ref):
        at = pos_ref[0]
        own_x, own_z, own_c = at // 8, (at // 2) % 4, at % 2
        tn = (((0,), (0,)), ((), ()))
        for yr in range(groups):
            k = yr ^ pos_ref[1]
            p_ref[...] = (
                lax.dot_general(r1_ref[k], s1_ref[...], tn, preferred_element_type=F32)
                + lax.dot_general(r2_ref[k], s2_ref[...], tn, preferred_element_type=F32)
            ) * scale
            for xr in range(X):
                for zr in range(Z):
                    base = (own_x ^ xr) * 8 + (own_z ^ zr) * 2
                    mine = p_ref[pl.ds((base + own_c) * rows_each, rows_each), :]
                    k0_ref[yr, xr, zr] = mine[:, :hc]
                    k1_ref[xr, yr, zr] = mine[:, hc:]
                    other = p_ref[pl.ds((base + (own_c ^ 1)) * rows_each, rows_each), :].astype(BF16)
                    t0_ref[yr, xr, zr] = other[:, :hc]
                    t1_ref[xr, yr, zr] = other[:, hc:]

    keep_y, keep_x, give_y, give_x = call(
        weight_body,
        [(keep_shape, F32), (keep_shape, F32), (keep_shape, BF16), (keep_shape, BF16)],
        [((C, C), F32)],
        ("S", pos), ("V", rows_1), ("V", slope_1), ("V", rows_2), ("V", slope_2),
    )
    part_y = keep_y + swap_space(give_y, 1).astype(F32)
    part_x = keep_x + swap_space(give_x, 1).astype(F32)

    def halve(a, swap, unit, dtype):
        got = swap(a[1:3].astype(dtype), unit).astype(F32)
        rest = swap((a[3] + got[1]).astype(dtype), 3 * unit).astype(F32)
        return (a[0] + got[0]) + rest

    def unpack_body(pos_ref, own_ref, first_ref, last_ref, o0, o1, o2, o3, t_ref):
        for b in range(NB):
            t_ref[b] = own_ref[b] + (first_ref[b] if b < R else last_ref[b - (NB - R)])
        for d, o in enumerate((o0, o1, o2, o3)):
            start = pl.multiple_of(m_own * (pos_ref[1] ^ d), m_own)
            for b in range(NB):
                o[b] = t_ref[b, pl.ds(start, m_own), :]

    pieces = call(
        unpack_body, [(piece, F32)] * 4, [(field, F32)],
        ("S", pos), ("V", own), ("V", to_next(hi)), ("V", to_prev(lo)),
    )
    part_y, part_x, pieces = lax.optimization_barrier((part_y, part_x, pieces))
    pieces = [pieces[0]] + [swap_member(pieces[d], d) for d in (1, 2, 3)]

    part_y = halve(part_y, swap_member, 1, BF16)
    part_x = halve(part_x, swap_space, 8, BF16)
    part_y, part_x, pieces = lax.optimization_barrier((part_y, part_x, pieces))
    part_y = halve(part_y, swap_space, 8, F32)
    part_x = halve(part_x, swap_member, 1, F32)
    part = halve(jnp.concatenate([part_y, part_x], axis=-1), swap_space, 2, F32)
    def finish_body(pos_ref, p0, p1, p2, p3, o_ref, t_ref):
        for d, r in enumerate((p0, p1, p2, p3)):
            t_ref[pl.ds(NB * (pos_ref[2] ^ d), NB)] = r[...]
        for b in range(b_own):
            o_ref[:, b, :] = t_ref[b]

    (grad,) = call(
        finish_body, [((m_own, b_own, C), F32)], [((b_own, m_own, C), F32)],
        ("S", pos), *[("V", p) for p in pieces],
    )

    part, grad = lax.optimization_barrier((part, grad))
    part = part + swap_window(part)
    near = swap_member(part, 1)
    pair = jnp.stack([part, near])
    far = swap_member(pair, 3)

    def rows_body(pos_ref, a_ref, f_ref, o_ref):
        o_ref[pos_ref[1]] = a_ref[0]
        o_ref[pos_ref[1] ^ 1] = a_ref[1]
        o_ref[pos_ref[1] ^ 3] = f_ref[0]
        o_ref[pos_ref[1] ^ 2] = f_ref[1]

    (weight_grad,) = call(
        rows_body, [((K, rows_each, C), F32)], [], ("S", pos), ("V", pair), ("V", far)
    )
    return weight_grad, grad[None]


def solution(mesh):
    in_specs = (
        P("window", "member", "space", None),
        P("window", None, "member", "space", None),
        P("window", None, "space", None),
        P("window", None, "space", None),
        P("space", None),
        P("space", None),
        P(),
        P("window", "member", "space", None),
    )
    out_specs = (P(None, "space", None), P("window", "member", "space", None))
    return jax.shard_map(local, mesh=mesh, in_specs=in_specs, out_specs=out_specs, check_vma=False)
```

```python
import math

import jax
import jax.numpy as jnp
from jax import lax
from jax.experimental import pallas as pl
from jax.experimental.pallas import tpu as pltpu
from jax.sharding import PartitionSpec as P

R = 2
INTERPRET = False
F32 = jnp.float32
BF16 = jnp.bfloat16
HI = lax.Precision.HIGHEST
VM = pl.BlockSpec(memory_space=pltpu.VMEM)
SM = pl.BlockSpec(memory_space=pltpu.SMEM)


def nn(a, b):
    return lax.dot_general(a, b, (((1,), (0,)), ((), ())), precision=HI, preferred_element_type=F32)


def nt(a, b):
    return lax.dot_general(a, b, (((1,), (1,)), ((), ())), precision=HI, preferred_element_type=F32)


def call(body, outs, scratch, *args):
    specs = {"S": SM, "V": VM}
    windowed = any(not isinstance(kind, str) for kind, _ in args)
    return pl.pallas_call(
        body,
        grid=(1,) if windowed else (),
        out_shape=[jax.ShapeDtypeStruct(s, d) for s, d in outs],
        in_specs=[specs[kind] if isinstance(kind, str) else kind for kind, _ in args],
        out_specs=[VM] * len(outs),
        scratch_shapes=[pltpu.VMEM(s, d) for s, d in scratch],
        interpret=INTERPRET,
    )(*[a for _, a in args])


def small_inverse(m):
    n = len(m)
    if n == 1:
        return [[1.0 / m[0][0]]]
    h = n // 2
    top = small_inverse([r[:h] for r in m[:h]])
    c = [r[:h] for r in m[h:]]
    ct = [[sum(c[i][p] * top[p][j] for p in range(h)) for j in range(h)] for i in range(h)]
    schur = [
        [m[h + i][h + j] - sum(ct[i][p] * c[j][p] for p in range(h)) for j in range(h)]
        for i in range(h)
    ]
    low = small_inverse(schur)
    cross = [[-sum(low[i][p] * ct[p][j] for p in range(h)) for j in range(h)] for i in range(h)]
    first = [
        [top[i][j] - sum(ct[p][i] * cross[p][j] for p in range(h)) for j in range(h)] for i in range(h)
    ]
    return [first[i] + [cross[p][i] for p in range(h)] for i in range(h)] + [
        cross[i] + low[i] for i in range(h)
    ]


def spd_inverse(a, step=4):
    n = a.shape[0]
    row_ids = lax.broadcasted_iota(jnp.int32, (n, n), 0)
    col_ids = lax.broadcasted_iota(jnp.int32, (n, n), 1)
    lane = lax.broadcasted_iota(jnp.int32, (1, n), 1)
    for k in range(0, n, step):
        at = range(k, k + step)
        cols = [jnp.broadcast_to(a[:, q : q + 1], (n, n)) for q in at]
        rows = [a[q : q + 1, :] for q in at]
        inv = small_inverse([[cols[q][p : p + 1, :] for q in range(step)] for p in at])
        a = jnp.where(col_ids // step == k // step, 0.0, a)
        for q in range(step):
            new = sum(inv[q][p] * rows[p] for p in range(step))
            for p in range(step):
                new = jnp.where(lane == k + p, -inv[q][p], new)
            new = jnp.broadcast_to(new, (n, n))
            a = a - cols[q] * new
            cols[q] = new
        for q in range(step):
            a = jnp.where(row_ids == k + q, cols[q], a)
    return -a


def local(
    initial_replica_fields,
    sensor_jitter,
    measurements,
    measured_indicator,
    sensor_error_power,
    adjacent_tiles,
    coupling_operators,
    analysis_cotangent,
):
    K, C = coupling_operators.shape[0], coupling_operators.shape[1]
    m_own, b_own = initial_replica_fields.shape[1], initial_replica_fields.shape[2]
    spaces, groups, windows = (lax.axis_size(a) for a in ("space", "member", "window"))
    N = m_own * groups
    NB = b_own // groups
    total = b_own * spaces
    spread = math.sqrt(N - 1.0)
    y = lax.axis_index("member").astype(jnp.int32)
    s = lax.axis_index("space").astype(jnp.int32)
    turn = groups - 1
    q = y ^ (turn * (s % 2))
    pos = jnp.stack([s, y, q])
    weights = coupling_operators.reshape(K * C, C)
    field = (NB, N, C)
    piece = (NB, m_own, C)
    half = (R, N, C)
    triple = (NB, 3, m_own, C)

    def swap_member(a, d):
        return lax.ppermute(a, "member", [(i, i ^ d) for i in range(groups)])

    def swap_space(a, d):
        return lax.ppermute(a, "space", [(i, i ^ d) for i in range(spaces)])

    def swap_window(a):
        return lax.ppermute(a, "window", [(i, i ^ 1) for i in range(windows)])

    order = [i * groups + (j ^ (turn * (i % 2))) for i in range(spaces) for j in range(groups)]
    ahead = order[1:] + order[:1]

    def to_next(a):
        return lax.ppermute(a, ("space", "member"), list(zip(order, ahead)))

    def to_prev(a):
        return lax.ppermute(a, ("space", "member"), list(zip(ahead, order)))

    def sum_all(a):
        for d in (1, 3):
            a = a + swap_member(a, d)
        for d in (1, 2, 6, 8, 24):
            a = a + swap_space(a, d)
        return a

    def pack(x, c):
        def body(pos_ref, x_ref, j_ref, o0, o1, o2, o3, t_ref):
            for b in range(b_own):
                v = x_ref[:, b, :]
                high = v.astype(BF16)
                t_ref[b, 0] = high
                t_ref[b, 1] = (v - high.astype(F32)).astype(BF16)
                t_ref[b, 2] = j_ref[0, :, b, :].astype(BF16)
            for d, o in enumerate((o0, o1, o2, o3)):
                o[...] = t_ref[pl.ds(NB * (pos_ref[2] ^ d), NB)]

        one_cycle = pl.BlockSpec((1, m_own, b_own, C), lambda i: (c, 0, 0, 0))
        pieces = call(
            body, [(triple, BF16)] * 4, [((b_own, 3, m_own, C), BF16)],
            ("S", pos), ("V", x), (one_cycle, sensor_jitter[0]),
        )
        return [pieces[0]] + [swap_member(pieces[d], d) for d in (1, 2, 3)]

    def merge(pieces, halos):
        def body(pos_ref, p0, p1, p2, p3, f_ref, j_ref, *rest):
            t_ref = rest[-1]
            for d, r in enumerate((p0, p1, p2, p3)):
                t_ref[pos_ref[1] ^ d] = r[...]
            for b in range(NB):
                high = t_ref[:, b, 0].reshape(N, C)
                f_ref[b] = high.astype(F32) + t_ref[:, b, 1].reshape(N, C).astype(F32)
                j_ref[b] = t_ref[:, b, 2].reshape(N, C)
                if halos:
                    rest[0 if b < R else 1][b % R] = high

        outs = [(field, F32), (field, BF16)] + ([(half, BF16)] * 2 if halos else [])
        return call(body, outs, [((groups,) + triple, BF16)], ("S", pos), *[("V", p) for p in pieces])

    prior_1, jitter_1, lo, hi = merge(pack(initial_replica_fields[0], 0), True)
    g_2, jitter_2 = merge(pack(analysis_cotangent[0], 1), False)

    def fold(m):
        return jnp.concatenate([m[: N // 2], m[N // 2 :]], axis=1)

    def unfold(m):
        return jnp.concatenate([m[:, :N], m[:, N:]], axis=0)

    def slot(pos_ref, adj_ref, b, k):
        b_here = NB * pos_ref[2] + b
        own = b_own * pos_ref[0] + b_here
        off = lax.rem(adj_ref[b_here, k] - own + total + total // 2, total) - total // 2
        return b + R + off

    def obs(pos_ref, mask_ref, err_ref, c, b):
        at = NB * pos_ref[2] + b
        mask = mask_ref[c, pl.ds(at, 1), :].astype(F32)
        inv_sd = 1.0 / jnp.sqrt(err_ref[pl.ds(at, 1), :])
        return mask, inv_sd

    def cell_pass(c, pos_ref, adj_ref, pad_ref, prior, w_ref, meas_ref, mask_ref, err_ref, j_ref,
                  rows_ref, grow_ref, an_ref, inn_ref, gc_ref, on_forecast, g_ref=None):
        acc = jnp.zeros((NB * N, C), F32)
        for k in range(K):
            for b in range(NB):
                rows_ref[k, b * N : (b + 1) * N, :] = pad_ref[slot(pos_ref, adj_ref, b, k)]
            acc = acc + jnp.dot(
                rows_ref[k], w_ref[k * C : (k + 1) * C, :], preferred_element_type=F32
            )
        growth = jnp.tanh(acc)
        sums = jnp.zeros((N, 2 * N), F32)
        cbar = jnp.zeros((N, N), F32)
        for b in range(NB):
            grow = growth[b * N : (b + 1) * N]
            fc = prior(b) + grow
            an = anomaly(fc)
            mask, inv_sd = obs(pos_ref, mask_ref, err_ref, c, b)
            sc = (mask * inv_sd) * an
            meas = meas_ref[c, pl.ds(NB * pos_ref[2] + b, 1), :]
            inn = mask * ((meas - fc) * inv_sd + j_ref[b].astype(F32))
            grow_ref[b] = grow
            an_ref[b] = an
            inn_ref[b] = inn
            on_forecast(b, fc)
            sums = sums + nt(sc, jnp.concatenate([sc, inn], axis=0))
            if g_ref is not None:
                cbar = cbar + nt(an, g_ref[b])
        gc_ref[0:N] = sums
        if g_ref is not None:
            gc_ref[N:] = fold(cbar)

    def anomaly(fc):
        return (fc - jnp.mean(fc, axis=0, keepdims=True)) / spread

    def first_body(pos_ref, adj_ref, mask_ref, err_ref, w_ref, meas_ref, j_ref, prev_ref, next_ref, prior_ref,
                   rows_ref, grow_ref, an_ref, inn_ref, gc_ref, lo_ref, hi_ref, pad_ref):
        pad_ref[0:R] = prev_ref[...]
        pad_ref[R : R + NB] = prior_ref[...].astype(BF16)
        pad_ref[R + NB :] = next_ref[...]

        def keep(b, fc):
            (lo_ref if b < R else hi_ref)[b % R] = fc

        cell_pass(0, pos_ref, adj_ref, pad_ref, lambda b: prior_ref[b], w_ref, meas_ref, mask_ref, err_ref,
                  j_ref, rows_ref, grow_ref, an_ref, inn_ref, gc_ref, keep)

    def second_body(pos_ref, adj_ref, mask_ref, err_ref, w_ref, meas_ref, j_ref, g_ref, gc1_ref, an1_ref,
                    lo_ref, hi_ref, prev_ref, next_ref,
                    rows_ref, grow_ref, an_ref, inn_ref, gc_ref, inv_ref, co_ref, pad_ref, prior_ref):
        inverse, coeff = solve(gc1_ref)
        inv_ref[...] = inverse
        co_ref[...] = coeff
        coeff_t = coeff.T
        for r in range(R):
            for at, ref in ((r, prev_ref), (R + NB + r, next_ref)):
                fc = ref[r]
                pad_ref[at] = (fc + nn(coeff_t, anomaly(fc))).astype(BF16)
        for b in range(NB):
            v = (lo_ref if b < R else hi_ref)[b % R] + nn(coeff_t, an1_ref[b])
            prior_ref[b] = v
            pad_ref[R + b] = v.astype(BF16)
        cell_pass(1, pos_ref, adj_ref, pad_ref, lambda b: prior_ref[b], w_ref, meas_ref, mask_ref, err_ref,
                  j_ref, rows_ref, grow_ref, an_ref, inn_ref, gc_ref, lambda b, fc: None, g_ref)

    def solve(gc_ref):
        ident = (
            lax.broadcasted_iota(jnp.int32, (N, N), 0) == lax.broadcasted_iota(jnp.int32, (N, N), 1)
        ).astype(F32)
        inverse = spd_inverse(ident + gc_ref[0:N, 0:N])
        return inverse, nn(inverse, gc_ref[0:N, N:])

    def backward(c, pos_ref, adj_ref, mask_ref, err_ref, w_ref, inverse, coeff, cbar, an_ref, inn_ref,
                 g_ref, grow_ref, slope_ref, own_ref, lo_ref, hi_ref, acc_ref):
        cross_bar = nn(inverse, cbar)
        gram_bar = -nt(cross_bar, coeff)
        sym = gram_bar + gram_bar.T

        def centered(m):
            return (m - jnp.mean(m, axis=0, keepdims=True)) / spread

        on_scaled = centered(sym) - cross_bar.T
        on_inn = centered(cross_bar)
        on_g = centered(coeff)
        acc_ref[...] = jnp.zeros(acc_ref.shape, F32)
        for b in range(NB):
            mask, inv_sd = obs(pos_ref, mask_ref, err_ref, c, b)
            weight = mask * inv_sd
            g = g_ref[b]
            fbar = g + nn(on_g, g) + weight * (
                nn(on_scaled, weight * an_ref[b]) + nn(on_inn, inn_ref[b])
            )
            grow = grow_ref[b]
            slope_ref[b * N : (b + 1) * N, :] = (fbar * (1.0 - grow * grow)).astype(BF16)
            acc_ref[R + b] = fbar
        for k in range(K):
            back = lax.dot_general(
                slope_ref[...], w_ref[k * C : (k + 1) * C, :], (((1,), (1,)), ((), ())),
                preferred_element_type=F32,
            )
            for b in range(NB):
                at = slot(pos_ref, adj_ref, b, k)
                acc_ref[at] = acc_ref[at] + back[b * N : (b + 1) * N]
        lo_ref[...] = acc_ref[0:R]
        own_ref[...] = acc_ref[R : R + NB]
        hi_ref[...] = acc_ref[R + NB :]

    back_outs = [((NB * N, C), BF16), (field, F32), (half, F32), (half, F32)]
    back_scratch = [((NB + 2 * R, N, C), F32)]

    def back_2_body(pos_ref, adj_ref, mask_ref, err_ref, w_ref, gc_ref, an_ref, inn_ref, g_ref, grow_ref,
                    an1_ref, prev_ref, next_ref, slope_ref, own_ref, lo_ref, hi_ref, cb_ref, acc_ref):
        inverse, coeff = solve(gc_ref)
        backward(1, pos_ref, adj_ref, mask_ref, err_ref, w_ref, inverse, coeff, unfold(gc_ref[N:]), an_ref,
                 inn_ref, g_ref, grow_ref, slope_ref, own_ref, lo_ref, hi_ref, acc_ref)

        cbar = jnp.zeros((N, N), F32)
        for b in range(NB):
            cbar = cbar + nt(an1_ref[b], acc_ref[R + b])
        for r in range(R):
            cbar = cbar + nt(anomaly(prev_ref[r]), acc_ref[r])
            cbar = cbar + nt(anomaly(next_ref[r]), acc_ref[R + NB + r])
        cb_ref[...] = fold(cbar)

    def back_1_body(pos_ref, adj_ref, mask_ref, err_ref, w_ref, inv_ref, co_ref, cb_ref, an_ref, inn_ref,
                    part_ref, first_ref, last_ref, grow_ref, slope_ref, own_ref, lo_ref, hi_ref, acc_ref,
                    g_ref):
        for b in range(NB):
            g_ref[b] = part_ref[b] + (first_ref[b] if b < R else last_ref[b - (NB - R)])
        backward(0, pos_ref, adj_ref, mask_ref, err_ref, w_ref, inv_ref[...], co_ref[...], unfold(cb_ref[...]),
                 an_ref, inn_ref, g_ref, grow_ref, slope_ref, own_ref, lo_ref, hi_ref, acc_ref)

    statics = [("S", pos), ("S", adjacent_tiles), ("V", measured_indicator[0]), ("V", sensor_error_power),
               ("V", weights)]

    rows_shape = ((K, NB * N, C), BF16)
    pad = ((NB + 2 * R, N, C), BF16)
    rows_1, grow_1, an_1, inn_1, gc_1, fc_lo, fc_hi = call(
        first_body,
        [rows_shape] + [(field, F32)] * 3 + [((N, 2 * N), F32)] + [(half, F32)] * 2,
        [pad],
        *statics, ("V", measurements[0]), ("V", jitter_1),
        ("V", to_next(hi)), ("V", to_prev(lo)), ("V", prior_1),
    )
    fc_prev, fc_next = to_next(fc_hi), to_prev(fc_lo)
    gc_1 = sum_all(gc_1)
    rows_2, grow_2, an_2, inn_2, gc_2, inv_1, co_1 = call(
        second_body,
        [rows_shape] + [(field, F32)] * 3 + [((3 * N // 2, 2 * N), F32)] + [((N, N), F32)] * 2,
        [pad, (field, F32)],
        *statics, ("V", measurements[0]), ("V", jitter_2), ("V", g_2), ("V", gc_1), ("V", an_1),
        ("V", fc_lo), ("V", fc_hi), ("V", fc_prev), ("V", fc_next),
    )
    gc_2 = sum_all(gc_2)
    slope_2, own, lo, hi, cb_1 = call(
        back_2_body, back_outs + [((N // 2, 2 * N), F32)], back_scratch, *statics,
        ("V", gc_2), ("V", an_2), ("V", inn_2), ("V", g_2), ("V", grow_2),
        ("V", an_1), ("V", fc_prev), ("V", fc_next),
    )
    first, last = to_next(hi), to_prev(lo)
    cb_1 = sum_all(cb_1)
    slope_1, own, lo, hi = call(
        back_1_body, back_outs, back_scratch + [(field, F32)], *statics,
        ("V", inv_1), ("V", co_1), ("V", cb_1), ("V", an_1), ("V", inn_1),
        ("V", own), ("V", first), ("V", last), ("V", grow_1),
    )
    first = to_next(hi)
    last = to_prev(lo)

    X, Z = 4, 4
    rows_each = C // spaces
    hc = C // 2
    keep_shape = (4, 4, Z, rows_each, hc)
    scale = 1.0 / math.sqrt(windows * N * total)

    def weight_body(pos_ref, r1_ref, s1_ref, r2_ref, s2_ref, k0_ref, k1_ref, t0_ref, t1_ref, p_ref):
        at = pos_ref[0]
        own_x, own_z, own_c = at // 8, (at // 2) % 4, at % 2
        tn = (((0,), (0,)), ((), ()))
        for yr in range(groups):
            k = yr ^ pos_ref[1]
            p_ref[...] = (
                lax.dot_general(r1_ref[k], s1_ref[...], tn, preferred_element_type=F32)
                + lax.dot_general(r2_ref[k], s2_ref[...], tn, preferred_element_type=F32)
            ) * scale
            for xr in range(X):
                for zr in range(Z):
                    base = (own_x ^ xr) * 8 + (own_z ^ zr) * 2
                    mine = p_ref[pl.ds((base + own_c) * rows_each, rows_each), :]
                    k0_ref[yr, xr, zr] = mine[:, :hc]
                    k1_ref[xr, yr, zr] = mine[:, hc:]
                    other = p_ref[pl.ds((base + (own_c ^ 1)) * rows_each, rows_each), :].astype(BF16)
                    t0_ref[yr, xr, zr] = other[:, :hc]
                    t1_ref[xr, yr, zr] = other[:, hc:]

    keep_y, keep_x, give_y, give_x = call(
        weight_body,
        [(keep_shape, F32), (keep_shape, F32), (keep_shape, BF16), (keep_shape, BF16)],
        [((C, C), F32)],
        ("S", pos), ("V", rows_1), ("V", slope_1), ("V", rows_2), ("V", slope_2),
    )
    part_y = keep_y + swap_space(give_y, 1).astype(F32)
    part_x = keep_x + swap_space(give_x, 1).astype(F32)

    def halve(a, swap, unit, dtype):
        got = swap(a[1:3].astype(dtype), unit).astype(F32)
        rest = swap((a[3] + got[1]).astype(dtype), 3 * unit).astype(F32)
        return (a[0] + got[0]) + rest

    def unpack_body(pos_ref, own_ref, first_ref, last_ref, o0, o1, o2, o3, t_ref):
        for b in range(NB):
            t_ref[b] = own_ref[b] + (first_ref[b] if b < R else last_ref[b - (NB - R)])
        for d, o in enumerate((o0, o1, o2, o3)):
            start = pl.multiple_of(m_own * (pos_ref[1] ^ d), m_own)
            for b in range(NB):
                o[b] = t_ref[b, pl.ds(start, m_own), :]

    pieces = call(
        unpack_body, [(piece, F32)] * 4, [(field, F32)],
        ("S", pos), ("V", own), ("V", first), ("V", last),
    )
    part_y, part_x, pieces = lax.optimization_barrier((part_y, part_x, pieces))
    pieces = [pieces[0]] + [swap_member(pieces[d], d) for d in (1, 2, 3)]

    part_y = halve(part_y, swap_member, 1, BF16)
    part_x = halve(part_x, swap_space, 8, BF16)
    part_y, part_x, pieces = lax.optimization_barrier((part_y, part_x, pieces))
    part_y = halve(part_y, swap_space, 8, F32)
    part_x = halve(part_x, swap_member, 1, F32)
    part = halve(jnp.concatenate([part_y, part_x], axis=-1), swap_space, 2, F32)

    def finish_body(pos_ref, p0, p1, p2, p3, o_ref, t_ref):
        for d, r in enumerate((p0, p1, p2, p3)):
            t_ref[pl.ds(NB * (pos_ref[2] ^ d), NB)] = r[...]
        for b in range(b_own):
            o_ref[:, b, :] = t_ref[b]

    (grad,) = call(
        finish_body, [((m_own, b_own, C), F32)], [((b_own, m_own, C), F32)],
        ("S", pos), *[("V", p) for p in pieces],
    )

    part, grad = lax.optimization_barrier((part, grad))
    part = part + swap_window(part)
    near = swap_member(part, 1)
    pair = jnp.stack([part, near])
    far = swap_member(pair, 3)

    def rows_body(pos_ref, a_ref, f_ref, o_ref):
        o_ref[pos_ref[1]] = a_ref[0]
        o_ref[pos_ref[1] ^ 1] = a_ref[1]
        o_ref[pos_ref[1] ^ 3] = f_ref[0]
        o_ref[pos_ref[1] ^ 2] = f_ref[1]

    (weight_grad,) = call(
        rows_body, [((K, rows_each, C), F32)], [], ("S", pos), ("V", pair), ("V", far)
    )
    return weight_grad, grad[None]


def solution(mesh):
    in_specs = (
        P("window", "member", "space", None),
        P("window", None, "member", "space", None),
        P("window", None, "space", None),
        P("window", None, "space", None),
        P("space", None),
        P("space", None),
        P(),
        P("window", "member", "space", None),
    )
    out_specs = (P(None, "space", None), P("window", "member", "space", None))
    return jax.shard_map(local, mesh=mesh, in_specs=in_specs, out_specs=out_specs, check_vma=False)
```

```python
import math

import jax
import jax.numpy as jnp
from jax import lax
from jax.experimental import pallas as pl
from jax.experimental.pallas import tpu as pltpu
from jax.sharding import PartitionSpec as P

R = 2
INTERPRET = False
F32 = jnp.float32
BF16 = jnp.bfloat16
HI = lax.Precision.HIGHEST
VM = pl.BlockSpec(memory_space=pltpu.VMEM)
SM = pl.BlockSpec(memory_space=pltpu.SMEM)


def nn(a, b):
    return lax.dot_general(a, b, (((1,), (0,)), ((), ())), precision=HI, preferred_element_type=F32)


def nt(a, b):
    return lax.dot_general(a, b, (((1,), (1,)), ((), ())), precision=HI, preferred_element_type=F32)


def call(body, outs, scratch, *args):
    specs = {"S": SM, "V": VM}
    windowed = any(not isinstance(kind, str) for kind, _ in args)
    return pl.pallas_call(
        body,
        grid=(1,) if windowed else (),
        out_shape=[jax.ShapeDtypeStruct(s, d) for s, d in outs],
        in_specs=[specs[kind] if isinstance(kind, str) else kind for kind, _ in args],
        out_specs=[VM] * len(outs),
        scratch_shapes=[pltpu.VMEM(s, d) for s, d in scratch],
        interpret=INTERPRET,
    )(*[a for _, a in args])


def small_inverse(m):
    n = len(m)
    if n == 1:
        return [[1.0 / m[0][0]]]
    h = n // 2
    top = small_inverse([r[:h] for r in m[:h]])
    c = [r[:h] for r in m[h:]]
    ct = [[sum(c[i][p] * top[p][j] for p in range(h)) for j in range(h)] for i in range(h)]
    schur = [
        [m[h + i][h + j] - sum(ct[i][p] * c[j][p] for p in range(h)) for j in range(h)]
        for i in range(h)
    ]
    low = small_inverse(schur)
    cross = [[-sum(low[i][p] * ct[p][j] for p in range(h)) for j in range(h)] for i in range(h)]
    first = [
        [top[i][j] - sum(ct[p][i] * cross[p][j] for p in range(h)) for j in range(h)] for i in range(h)
    ]
    return [first[i] + [cross[p][i] for p in range(h)] for i in range(h)] + [
        cross[i] + low[i] for i in range(h)
    ]


def spd_inverse(a, step=4):
    n = a.shape[0]
    row_ids = lax.broadcasted_iota(jnp.int32, (n, n), 0)
    col_ids = lax.broadcasted_iota(jnp.int32, (n, n), 1)
    lane = lax.broadcasted_iota(jnp.int32, (1, n), 1)
    for k in range(0, n, step):
        at = range(k, k + step)
        cols = [jnp.broadcast_to(a[:, q : q + 1], (n, n)) for q in at]
        rows = [a[q : q + 1, :] for q in at]
        inv = small_inverse([[cols[q][p : p + 1, :] for q in range(step)] for p in at])
        a = jnp.where(col_ids // step == k // step, 0.0, a)
        for q in range(step):
            new = sum(inv[q][p] * rows[p] for p in range(step))
            for p in range(step):
                new = jnp.where(lane == k + p, -inv[q][p], new)
            new = jnp.broadcast_to(new, (n, n))
            a = a - cols[q] * new
            cols[q] = new
        for q in range(step):
            a = jnp.where(row_ids == k + q, cols[q], a)
    return -a


def local(
    initial_replica_fields,
    sensor_jitter,
    measurements,
    measured_indicator,
    sensor_error_power,
    adjacent_tiles,
    coupling_operators,
    analysis_cotangent,
):
    K, C = coupling_operators.shape[0], coupling_operators.shape[1]
    m_own, b_own = initial_replica_fields.shape[1], initial_replica_fields.shape[2]
    spaces, groups, windows = (lax.axis_size(a) for a in ("space", "member", "window"))
    N = m_own * groups
    NB = b_own // groups
    total = b_own * spaces
    spread = math.sqrt(N - 1.0)
    y = lax.axis_index("member").astype(jnp.int32)
    s = lax.axis_index("space").astype(jnp.int32)
    turn = groups - 1
    q = y ^ (turn * (s % 2))
    pos = jnp.stack([s, y, q])
    weights = coupling_operators.reshape(K * C, C)
    field = (NB, N, C)
    piece = (NB, m_own, C)
    half = (R, N, C)
    triple = (NB, 3, m_own, C)

    def swap_member(a, d):
        return lax.ppermute(a, "member", [(i, i ^ d) for i in range(groups)])

    def swap_space(a, d):
        return lax.ppermute(a, "space", [(i, i ^ d) for i in range(spaces)])

    def swap_window(a):
        return lax.ppermute(a, "window", [(i, i ^ 1) for i in range(windows)])

    order = [i * groups + (j ^ (turn * (i % 2))) for i in range(spaces) for j in range(groups)]
    ahead = order[1:] + order[:1]

    def to_next(a):
        return lax.ppermute(a, ("space", "member"), list(zip(order, ahead)))

    def to_prev(a):
        return lax.ppermute(a, ("space", "member"), list(zip(ahead, order)))

    def sum_all(a):
        for d in (1, 2, 6, 8, 24):
            got = swap_space(a, d)
            a = a + got
        for d in (1, 3):
            got = swap_member(a, d)
            a = a + got
        return a

    def pack(x, c):
        def body(pos_ref, x_ref, j_ref, o0, o1, o2, o3, t_ref):
            for b in range(b_own):
                v = x_ref[:, b, :]
                high = v.astype(BF16)
                t_ref[b, 0] = high
                t_ref[b, 1] = (v - high.astype(F32)).astype(BF16)
                t_ref[b, 2] = j_ref[0, :, b, :].astype(BF16)
            for d, o in enumerate((o0, o1, o2, o3)):
                o[...] = t_ref[pl.ds(NB * (pos_ref[2] ^ d), NB)]

        one_cycle = pl.BlockSpec((1, m_own, b_own, C), lambda i: (c, 0, 0, 0))
        pieces = call(
            body, [(triple, BF16)] * 4, [((b_own, 3, m_own, C), BF16)],
            ("S", pos), ("V", x), (one_cycle, sensor_jitter[0]),
        )
        got = [pieces[0]]
        for d in (1, 2, 3):
            got.append(swap_member(pieces[d], d))
        return got

    def merge(pieces, halos):
        def body(pos_ref, p0, p1, p2, p3, f_ref, j_ref, *rest):
            t_ref = rest[-1]
            for d, r in enumerate((p0, p1, p2, p3)):
                t_ref[pos_ref[1] ^ d] = r[...]
            for b in range(NB):
                high = t_ref[:, b, 0].reshape(N, C)
                f_ref[b] = high.astype(F32) + t_ref[:, b, 1].reshape(N, C).astype(F32)
                j_ref[b] = t_ref[:, b, 2].reshape(N, C)
                if halos:
                    rest[0 if b < R else 1][b % R] = high

        outs = [(field, F32), (field, BF16)] + ([(half, BF16)] * 2 if halos else [])
        return call(body, outs, [((groups,) + triple, BF16)], ("S", pos), *[("V", p) for p in pieces])

    prior_1, jitter_1, lo, hi = merge(pack(initial_replica_fields[0], 0), True)
    g_2, jitter_2 = merge(pack(analysis_cotangent[0], 1), False)
    from_prev = to_next(hi)
    from_next = to_prev(lo)

    def fold(m):
        return jnp.concatenate([m[: N // 2], m[N // 2 :]], axis=1)

    def unfold(m):
        return jnp.concatenate([m[:, :N], m[:, N:]], axis=0)

    def slot(pos_ref, adj_ref, b, k):
        b_here = NB * pos_ref[2] + b
        own = b_own * pos_ref[0] + b_here
        off = lax.rem(adj_ref[b_here, k] - own + total + total // 2, total) - total // 2
        return b + R + off

    def obs(pos_ref, mask_ref, err_ref, c, b):
        at = NB * pos_ref[2] + b
        mask = mask_ref[c, pl.ds(at, 1), :].astype(F32)
        inv_sd = 1.0 / jnp.sqrt(err_ref[pl.ds(at, 1), :])
        return mask, inv_sd

    def cell_pass(c, pos_ref, adj_ref, pad_ref, prior, w_ref, meas_ref, mask_ref, err_ref, j_ref,
                  rows_ref, grow_ref, an_ref, inn_ref, gc_ref, on_forecast, g_ref=None):
        acc = jnp.zeros((NB * N, C), F32)
        for k in range(K):
            for b in range(NB):
                rows_ref[k, b * N : (b + 1) * N, :] = pad_ref[slot(pos_ref, adj_ref, b, k)]
            acc = acc + jnp.dot(
                rows_ref[k], w_ref[k * C : (k + 1) * C, :], preferred_element_type=F32
            )
        growth = jnp.tanh(acc)
        sums = jnp.zeros((N, 2 * N), F32)
        cbar = jnp.zeros((N, N), F32)
        for b in range(NB):
            grow = growth[b * N : (b + 1) * N]
            fc = prior(b) + grow
            an = anomaly(fc)
            mask, inv_sd = obs(pos_ref, mask_ref, err_ref, c, b)
            sc = (mask * inv_sd) * an
            meas = meas_ref[c, pl.ds(NB * pos_ref[2] + b, 1), :]
            inn = mask * ((meas - fc) * inv_sd + j_ref[b].astype(F32))
            grow_ref[b] = grow
            an_ref[b] = an
            inn_ref[b] = inn
            on_forecast(b, fc)
            sums = sums + nt(sc, jnp.concatenate([sc, inn], axis=0))
            if g_ref is not None:
                cbar = cbar + nt(an, g_ref[b])
        gc_ref[0:N] = sums
        if g_ref is not None:
            gc_ref[N:] = fold(cbar)

    def anomaly(fc):
        return (fc - jnp.mean(fc, axis=0, keepdims=True)) / spread

    def first_body(pos_ref, adj_ref, mask_ref, err_ref, w_ref, meas_ref, j_ref, prev_ref, next_ref, prior_ref,
                   rows_ref, grow_ref, an_ref, inn_ref, gc_ref, lo_ref, hi_ref, pad_ref):
        pad_ref[0:R] = prev_ref[...]
        pad_ref[R : R + NB] = prior_ref[...].astype(BF16)
        pad_ref[R + NB :] = next_ref[...]

        def keep(b, fc):
            (lo_ref if b < R else hi_ref)[b % R] = fc

        cell_pass(0, pos_ref, adj_ref, pad_ref, lambda b: prior_ref[b], w_ref, meas_ref, mask_ref, err_ref,
                  j_ref, rows_ref, grow_ref, an_ref, inn_ref, gc_ref, keep)

    def second_body(pos_ref, adj_ref, mask_ref, err_ref, w_ref, meas_ref, j_ref, g_ref, gc1_ref, an1_ref,
                    lo_ref, hi_ref, prev_ref, next_ref,
                    rows_ref, grow_ref, an_ref, inn_ref, gc_ref, inv_ref, co_ref, pad_ref, prior_ref):
        inverse, coeff = solve(gc1_ref)
        inv_ref[...] = inverse
        co_ref[...] = coeff
        coeff_t = coeff.T
        for r in range(R):
            for at, ref in ((r, prev_ref), (R + NB + r, next_ref)):
                fc = ref[r]
                pad_ref[at] = (fc + nn(coeff_t, anomaly(fc))).astype(BF16)
        for b in range(NB):
            v = (lo_ref if b < R else hi_ref)[b % R] + nn(coeff_t, an1_ref[b])
            prior_ref[b] = v
            pad_ref[R + b] = v.astype(BF16)
        cell_pass(1, pos_ref, adj_ref, pad_ref, lambda b: prior_ref[b], w_ref, meas_ref, mask_ref, err_ref,
                  j_ref, rows_ref, grow_ref, an_ref, inn_ref, gc_ref, lambda b, fc: None, g_ref)

    def solve(gc_ref):
        ident = (
            lax.broadcasted_iota(jnp.int32, (N, N), 0) == lax.broadcasted_iota(jnp.int32, (N, N), 1)
        ).astype(F32)
        inverse = spd_inverse(ident + gc_ref[0:N, 0:N])
        return inverse, nn(inverse, gc_ref[0:N, N:])

    def backward(c, pos_ref, adj_ref, mask_ref, err_ref, w_ref, inverse, coeff, cbar, an_ref, inn_ref,
                 g_ref, grow_ref, slope_ref, own_ref, lo_ref, hi_ref, acc_ref):
        cross_bar = nn(inverse, cbar)
        gram_bar = -nt(cross_bar, coeff)
        sym = gram_bar + gram_bar.T

        def centered(m):
            return (m - jnp.mean(m, axis=0, keepdims=True)) / spread

        on_cells = jnp.concatenate([centered(sym) - cross_bar.T, centered(cross_bar)], axis=1)
        on_g = centered(coeff)
        acc_ref[...] = jnp.zeros(acc_ref.shape, F32)
        for b in range(NB):
            mask, inv_sd = obs(pos_ref, mask_ref, err_ref, c, b)
            weight = mask * inv_sd
            g = g_ref[b]
            cells = jnp.concatenate([weight * an_ref[b], inn_ref[b]], axis=0)
            fbar = g + nn(on_g, g) + weight * nn(on_cells, cells)
            grow = grow_ref[b]
            slope_ref[b * N : (b + 1) * N, :] = (fbar * (1.0 - grow * grow)).astype(BF16)
            acc_ref[R + b] = fbar
        for k in range(K):
            back = lax.dot_general(
                slope_ref[...], w_ref[k * C : (k + 1) * C, :], (((1,), (1,)), ((), ())),
                preferred_element_type=F32,
            )
            for b in range(NB):
                at = slot(pos_ref, adj_ref, b, k)
                acc_ref[at] = acc_ref[at] + back[b * N : (b + 1) * N]
        lo_ref[...] = acc_ref[0:R]
        own_ref[...] = acc_ref[R : R + NB]
        hi_ref[...] = acc_ref[R + NB :]

    back_outs = [((NB * N, C), BF16), (field, F32), (half, F32), (half, F32)]
    back_scratch = [((NB + 2 * R, N, C), F32)]

    def back_2_body(pos_ref, adj_ref, mask_ref, err_ref, w_ref, gc_ref, an_ref, inn_ref, g_ref, grow_ref,
                    an1_ref, prev_ref, next_ref, slope_ref, own_ref, lo_ref, hi_ref, cb_ref, acc_ref):
        inverse, coeff = solve(gc_ref)
        backward(1, pos_ref, adj_ref, mask_ref, err_ref, w_ref, inverse, coeff, unfold(gc_ref[N:]), an_ref,
                 inn_ref, g_ref, grow_ref, slope_ref, own_ref, lo_ref, hi_ref, acc_ref)

        cbar = jnp.zeros((N, N), F32)
        for b in range(NB):
            cbar = cbar + nt(an1_ref[b], acc_ref[R + b])
        for r in range(R):
            cbar = cbar + nt(anomaly(prev_ref[r]), acc_ref[r])
            cbar = cbar + nt(anomaly(next_ref[r]), acc_ref[R + NB + r])
        cb_ref[...] = fold(cbar)

    def back_1_body(pos_ref, adj_ref, mask_ref, err_ref, w_ref, inv_ref, co_ref, cb_ref, an_ref, inn_ref,
                    part_ref, first_ref, last_ref, grow_ref, slope_ref, own_ref, lo_ref, hi_ref, acc_ref,
                    g_ref):
        for b in range(NB):
            g_ref[b] = part_ref[b] + (first_ref[b] if b < R else last_ref[b - (NB - R)])
        backward(0, pos_ref, adj_ref, mask_ref, err_ref, w_ref, inv_ref[...], co_ref[...], unfold(cb_ref[...]),
                 an_ref, inn_ref, g_ref, grow_ref, slope_ref, own_ref, lo_ref, hi_ref, acc_ref)

    statics = [("S", pos), ("S", adjacent_tiles), ("V", measured_indicator[0]), ("V", sensor_error_power),
               ("V", weights)]

    rows_shape = ((K, NB * N, C), BF16)
    pad = ((NB + 2 * R, N, C), BF16)
    rows_1, grow_1, an_1, inn_1, gc_1, fc_lo, fc_hi = call(
        first_body,
        [rows_shape] + [(field, F32)] * 3 + [((N, 2 * N), F32)] + [(half, F32)] * 2,
        [pad],
        *statics, ("V", measurements[0]), ("V", jitter_1),
        ("V", from_prev), ("V", from_next), ("V", prior_1),
    )
    fc_prev = to_next(fc_hi)
    fc_next = to_prev(fc_lo)
    gc_1 = sum_all(gc_1)
    rows_2, grow_2, an_2, inn_2, gc_2, inv_1, co_1 = call(
        second_body,
        [rows_shape] + [(field, F32)] * 3 + [((3 * N // 2, 2 * N), F32)] + [((N, N), F32)] * 2,
        [pad, (field, F32)],
        *statics, ("V", measurements[0]), ("V", jitter_2), ("V", g_2), ("V", gc_1), ("V", an_1),
        ("V", fc_lo), ("V", fc_hi), ("V", fc_prev), ("V", fc_next),
    )
    gc_2 = sum_all(gc_2)
    slope_2, own, lo, hi, cb_1 = call(
        back_2_body, back_outs + [((N // 2, 2 * N), F32)], back_scratch, *statics,
        ("V", gc_2), ("V", an_2), ("V", inn_2), ("V", g_2), ("V", grow_2),
        ("V", an_1), ("V", fc_prev), ("V", fc_next),
    )
    first = to_next(hi)
    last = to_prev(lo)
    cb_1 = sum_all(cb_1)
    slope_1, own, lo, hi = call(
        back_1_body, back_outs, back_scratch + [(field, F32)], *statics,
        ("V", inv_1), ("V", co_1), ("V", cb_1), ("V", an_1), ("V", inn_1),
        ("V", own), ("V", first), ("V", last), ("V", grow_1),
    )
    first = to_next(hi)
    last = to_prev(lo)

    X, Z = 4, 4
    rows_each = C // spaces
    hc = C // 2
    keep_shape = (4, 4, Z, rows_each, hc)
    scale = 1.0 / math.sqrt(windows * N * total)

    def weight_body(pos_ref, r1_ref, s1_ref, r2_ref, s2_ref, k0_ref, k1_ref, t0_ref, t1_ref, p_ref):
        at = pos_ref[0]
        own_x, own_z, own_c = at // 8, (at // 2) % 4, at % 2
        tn = (((0,), (0,)), ((), ()))
        for yr in range(groups):
            k = yr ^ pos_ref[1]
            p_ref[...] = (
                lax.dot_general(r1_ref[k], s1_ref[...], tn, preferred_element_type=F32)
                + lax.dot_general(r2_ref[k], s2_ref[...], tn, preferred_element_type=F32)
            ) * scale
            for xr in range(X):
                for zr in range(Z):
                    base = (own_x ^ xr) * 8 + (own_z ^ zr) * 2
                    mine = p_ref[pl.ds((base + own_c) * rows_each, rows_each), :]
                    k0_ref[yr, xr, zr] = mine[:, :hc]
                    k1_ref[xr, yr, zr] = mine[:, hc:]
                    other = p_ref[pl.ds((base + (own_c ^ 1)) * rows_each, rows_each), :].astype(BF16)
                    t0_ref[yr, xr, zr] = other[:, :hc]
                    t1_ref[xr, yr, zr] = other[:, hc:]

    keep_y, keep_x, give_y, give_x = call(
        weight_body,
        [(keep_shape, F32), (keep_shape, F32), (keep_shape, BF16), (keep_shape, BF16)],
        [((C, C), F32)],
        ("S", pos), ("V", rows_1), ("V", slope_1), ("V", rows_2), ("V", slope_2),
    )
    part_y = keep_y + swap_space(give_y, 1).astype(F32)
    part_x = keep_x + swap_space(give_x, 1).astype(F32)

    def halve(a, swap, unit, dtype):
        got = swap(a[1:3].astype(dtype), unit).astype(F32)
        rest = swap((a[3] + got[1]).astype(dtype), 3 * unit).astype(F32)
        return (a[0] + got[0]) + rest

    def unpack_body(pos_ref, own_ref, first_ref, last_ref, o0, o1, o2, o3, t_ref):
        for b in range(NB):
            t_ref[b] = own_ref[b] + (first_ref[b] if b < R else last_ref[b - (NB - R)])
        for d, o in enumerate((o0, o1, o2, o3)):
            start = pl.multiple_of(m_own * (pos_ref[1] ^ d), m_own)
            for b in range(NB):
                o[b] = t_ref[b, pl.ds(start, m_own), :]

    pieces = call(
        unpack_body, [(piece, F32)] * 4, [(field, F32)],
        ("S", pos), ("V", own), ("V", first), ("V", last),
    )
    part_y, part_x, pieces = lax.optimization_barrier((part_y, part_x, pieces))

    part_y = halve(part_y, swap_member, 1, BF16)
    part_x = halve(part_x, swap_space, 8, BF16)
    part_y, part_x, pieces = lax.optimization_barrier((part_y, part_x, pieces))
    back = [pieces[0]]
    for d in (1, 2, 3):
        back.append(swap_member(pieces[d], d))
    pieces = back
    part_y = halve(part_y, swap_space, 8, F32)
    part_x = halve(part_x, swap_member, 1, F32)
    part = halve(jnp.concatenate([part_y, part_x], axis=-1), swap_space, 2, F32)

    def finish_body(pos_ref, p0, p1, p2, p3, o_ref, t_ref):
        for d, r in enumerate((p0, p1, p2, p3)):
            t_ref[pl.ds(NB * (pos_ref[2] ^ d), NB)] = r[...]
        for b in range(b_own):
            o_ref[:, b, :] = t_ref[b]

    (grad,) = call(
        finish_body, [((m_own, b_own, C), F32)], [((b_own, m_own, C), F32)],
        ("S", pos), *[("V", p) for p in pieces],
    )

    part = part + swap_window(part)
    part, grad = lax.optimization_barrier((part, grad))
    near = swap_member(part, 1)
    pair = jnp.stack([part, near])
    far = swap_member(pair, 3)

    def rows_body(pos_ref, a_ref, f_ref, o_ref):
        o_ref[pos_ref[1]] = a_ref[0]
        o_ref[pos_ref[1] ^ 1] = a_ref[1]
        o_ref[pos_ref[1] ^ 3] = f_ref[0]
        o_ref[pos_ref[1] ^ 2] = f_ref[1]

    (weight_grad,) = call(
        rows_body, [((K, rows_each, C), F32)], [], ("S", pos), ("V", pair), ("V", far)
    )
    return weight_grad, grad[None]


def solution(mesh):
    in_specs = (
        P("window", "member", "space", None),
        P("window", None, "member", "space", None),
        P("window", None, "space", None),
        P("window", None, "space", None),
        P("space", None),
        P("space", None),
        P(),
        P("window", "member", "space", None),
    )
    out_specs = (P(None, "space", None), P("window", "member", "space", None))
    return jax.shard_map(local, mesh=mesh, in_specs=in_specs, out_specs=out_specs, check_vma=False)
```
